1024 devices in a mesh: ctx: 32 (over y, x), pp: 2 (over core), tp: 16 (over z).
Axes of the slice: x: 4, y: 8, z: 16, core: 2. Of those that a mesh axis runs over, the one named last changes fastest.
Arguments:
- outgoing: bfloat16 [2, 4096, 7168], P('pp', 'ctx', 'tp'), may hold values from -6 to 6
- w_down: bfloat16 [2, 7168, 576], P('pp', 'tp'), may hold values from -0.0625 to 0.0625
- kv_gain: float32 [2, 512], P('pp'), may hold values from 0.5 to 1.5
- queries: bfloat16 [2, 4096, 64, 192], P('pp', 'ctx', 'tp'), may hold values from -160 to 160
- w_key_up: bfloat16 [2, 64, 128, 512], P('pp', 'tp'), may hold values from -0.5 to 0.5
- w_value_up: bfloat16 [2, 64, 512, 128], P('pp', 'tp'), may hold values from -0.25 to 0.25
- block_ids: int32 [64], replicated, may hold values from 0 to 63, as said below
Outputs:
- heads_out: bfloat16 [2, 4096, 8192], P('pp', 'ctx', 'tp')
The draws below stay inside these ranges and needn't reach their ends.
Inputs may be any that keep to these rules, and one draw needn't show every extreme that they name: `block_ids`: each number appears once; index d of ctx holds the pair k and 63 - k for some k, in either order.
All inputs are finite; a program needn't handle non-finite values.
Results may differ from the reference program's by a relative error of at most 0.02.
Values may be sent and summed in bfloat16 or wider, within the bound.
No kernel may reach another device: no remote copies, remote signals or barrier semaphores. Data moves between devices by JAX's collectives and lax.ppermute only.
A program may use at most 32 MiB of HBM per device.

```python
import jax
import jax.numpy as jnp
from jax import lax

D = 7168
HEADS = 64
NOPE = 128
ROPE = 64
LATENT = 512
VHEAD = 128
TOK_DEV = 128
TOKENS = 4096
SECTIONS = 2
N_CTX = 32
N_TP = 16


def draw_block_ids(key, part):
    first_key, second_key = jax.random.split(jax.random.fold_in(key, 17))
    order = jax.random.permutation(first_key, N_CTX).astype(jnp.int32)
    flipped = jax.random.randint(second_key, (N_CTX,), 0, 2).astype(jnp.int32)
    early = jnp.where(flipped == 1, 2 * N_CTX - 1 - order, order)
    late = 2 * N_CTX - 1 - early
    return jnp.stack([early, late], axis=1).reshape(2 * N_CTX).astype(jnp.int32)


def draw_queries(key, part):
    base_key = jax.random.fold_in(jax.random.fold_in(key, 29), 0)
    full_shape = (SECTIONS, TOKENS, HEADS, NOPE + ROPE)
    values = jnp.clip(jax.random.normal(base_key, full_shape, jnp.float32), -6.0, 6.0)
    return values.astype(jnp.bfloat16)


def level_of(rng, dims, shards, least, high):
    gain, own = 1.0, jax.random.fold_in(rng, 6)
    for dim, shards_of in shards:
        steps = jnp.exp(jax.random.uniform(jax.random.fold_in(own, dim), (shards_of,), jnp.float32, least / len(shards), high / len(shards)))
        gain = gain * jnp.repeat(steps, dims[dim] // shards_of).reshape([-1 if axis == dim else 1 for axis in range(len(dims))])
    return gain


def normal_values(key, dims, deviation, reach, cuts=(), kind=jnp.bfloat16):
    entries = deviation * jax.random.normal(key, dims, jnp.float32)
    if cuts:
        entries = entries * level_of(key, dims, cuts, -0.22, 0.18)
    return jnp.clip(entries, -reach, reach).astype(kind)


def setup_inputs(seed: int = 0) -> dict:
    keys = jax.random.split(jax.random.key(seed), 8)
    return {
        "outgoing": normal_values(keys[0], (SECTIONS, TOKENS, D), 1.0, 6.0, ((0, 2), (1, 32), (2, 16))),
        "w_down": normal_values(keys[1], (SECTIONS, D, LATENT + ROPE), D ** -0.5, 0.0625, ((0, 2), (1, 16))),
        "kv_gain": jnp.clip(1.0 + 0.1 * jax.random.normal(keys[2], (SECTIONS, LATENT), jnp.float32), 0.5, 1.5),
        "queries": draw_queries(jax.random.fold_in(keys[7], 71), 0),
        "w_key_up": normal_values(keys[4], (SECTIONS, HEADS, NOPE, LATENT), NOPE ** -0.5, 0.5, ((0, 2), (1, 16))),
        "w_value_up": normal_values(keys[5], (SECTIONS, HEADS, LATENT, VHEAD), LATENT ** -0.5, 0.25, ((0, 2), (1, 16))),
        "block_ids": draw_block_ids(jax.random.fold_in(keys[7], 71), 0),
    }


def token_positions(table, count, half_len):
    token_idx = jnp.arange(count, dtype=jnp.int32)
    owner = token_idx // (2 * half_len)
    within = token_idx % (2 * half_len)
    slot_idx = 2 * owner + within // half_len
    return table[slot_idx] * half_len + within % half_len

def one_section(section_in, down_w, gain_row, query, key_up, value_up, table):
    raw_latent = jnp.dot(section_in, down_w, preferred_element_type=jnp.float32)
    latent_part = raw_latent[:, :LATENT]
    mean_sq = lax.optimization_barrier(jnp.mean(latent_part * latent_part, axis=-1, keepdims=True))
    normed = latent_part * lax.rsqrt(mean_sq + 1e-06) * gain_row
    key_rows = jnp.concatenate([normed, raw_latent[:, LATENT:]], axis=-1).astype(jnp.bfloat16)
    position = token_positions(table, TOKENS, TOK_DEV // 2)
    query_latent = jnp.einsum('thd,hdc->thc', query[..., :NOPE].astype(jnp.float32), key_up.astype(jnp.float32)).astype(jnp.bfloat16)
    query_full = jnp.concatenate([query_latent, query[..., NOPE:]], axis=-1)
    query_full = lax.optimization_barrier(query_full)
    group_size = HEADS // N_TP
    grouped = query_full.reshape(TOKENS, HEADS // group_size, group_size, LATENT + ROPE).transpose(1, 0, 2, 3)
    key_float = key_rows.astype(jnp.float32)
    value_float = key_rows[:, :LATENT].astype(jnp.float32)
    visible = position[None, :] <= position[:, None]
    score_scale = 1.0 / jnp.sqrt(jnp.float32(NOPE + ROPE))

    def head_group(query_group):
        scores = jnp.einsum('tgc,kc->tgk', query_group.astype(jnp.float32), key_float) * score_scale
        scores = jnp.where(visible[:, None, :], scores, jnp.float32(-1e+30))
        row_max = lax.optimization_barrier(jnp.max(scores, axis=-1, keepdims=True))
        expo = jnp.where(visible[:, None, :], jnp.exp(scores - row_max), jnp.float32(0.0))
        row_sum = lax.optimization_barrier(jnp.sum(expo, axis=-1, keepdims=True))
        attn_weights = expo.astype(jnp.bfloat16)
        attn_weights = lax.optimization_barrier(attn_weights)
        attended = jnp.einsum('tgk,kc->tgc', attn_weights.astype(jnp.float32), value_float) / row_sum
        return attended.astype(jnp.bfloat16)
    attended = lax.map(head_group, grouped)
    attended = lax.optimization_barrier(attended)
    attended = attended.transpose(1, 0, 2, 3).reshape(TOKENS, HEADS, LATENT)
    heads_out = jnp.einsum('thc,hcv->thv', attended.astype(jnp.float32), value_up.astype(jnp.float32))
    return heads_out.astype(jnp.bfloat16).reshape(TOKENS, HEADS * VHEAD)

def reference(outgoing, w_down, kv_gain, queries, w_key_up, w_value_up, block_ids):
    section_in = jnp.concatenate([outgoing[:1], outgoing[:-1]], axis=0)

    def run(items):
        return one_section(items[0], items[1], items[2], items[3], items[4], items[5], block_ids)
    return lax.map(run, (section_in, w_down, kv_gain, queries, w_key_up, w_value_up))
```

```python
import functools

import jax
import jax.numpy as jnp
from jax import lax
from jax.experimental import pallas as pl
from jax.experimental.pallas import tpu as pltpu
from jax.sharding import Mesh
from jax.sharding import PartitionSpec as P

CTX = ("y1", "y0", "x")
SHARE = ("y0", "x")
KEYS = ("y1",)
LANES = 128
LOG2_E = 1.4426950408889634
LOW = -1e30
WHOLE = pl.BlockSpec(memory_space=pltpu.VMEM)
SCALARS = pl.BlockSpec(memory_space=pltpu.SMEM)


def exchange(array, axes):
    return lax.all_to_all(array, axes, 0, 0, tiled=True)


def cost(flops, bytes_accessed):
    return pl.CostEstimate(flops=flops, bytes_accessed=bytes_accessed, transcendentals=0)


def pack_queries(query, copies):
    tokens, heads, width = query.shape
    nope = LANES
    rope = width - nope
    slabs = heads + heads * rope // LANES

    def kernel(query_ref, out_ref):
        rows = query_ref[...]
        for head in range(heads):
            slab = rows[:, head, :nope]
            for copy in range(copies):
                out_ref[copy, head] = slab
        for pair in range(heads // 2):
            slab = jnp.concatenate(
                [rows[:, 2 * pair, nope:], rows[:, 2 * pair + 1, nope:]], axis=-1
            )
            for copy in range(copies):
                out_ref[copy, heads + pair] = slab

    return pl.pallas_call(
        kernel,
        out_shape=jax.ShapeDtypeStruct((copies, slabs, tokens, LANES), query.dtype),
        in_specs=[WHOLE],
        out_specs=WHOLE,
        cost_estimate=cost(0, copies * slabs * tokens * LANES * 2),
        name="pack_queries",
    )(query)


def norm_rows(pieces, gain, copies):
    parts, rows, width = pieces.shape
    latent = gain.shape[-1]

    def kernel(pieces_ref, gain_ref, out_ref):
        raw = pieces_ref[0]
        for part in range(1, parts):
            raw = raw + pieces_ref[part]
        latent_part = raw[:, :latent]
        mean_sq = jnp.mean(latent_part * latent_part, axis=-1, keepdims=True)
        normed = latent_part * lax.rsqrt(mean_sq + 1e-06) * gain_ref[...]
        pad = jnp.zeros((rows, LANES - (width - latent)), jnp.float32)
        row = jnp.concatenate([normed, raw[:, latent:], pad], axis=-1).astype(jnp.bfloat16)
        for copy in range(copies):
            out_ref[copy] = row

    return pl.pallas_call(
        kernel,
        out_shape=jax.ShapeDtypeStruct((copies, rows, latent + LANES), jnp.bfloat16),
        in_specs=[WHOLE, WHOLE],
        out_specs=WHOLE,
        cost_estimate=cost(0, parts * rows * width * 8),
        name="norm_rows",
    )(pieces, gain)


def absorb(block_ids, place, slabs, key_up):
    share, n_slabs, tokens, _ = slabs.shape
    heads, _, latent = key_up.shape
    half = tokens // 2
    n_blocks = block_ids.shape[0]

    def kernel(ids_ref, place_ref, slab_ref, up_ref, out_ref):
        owner = place_ref[0] + pl.program_id(0)
        first = (ids_ref[2 * owner] >= n_blocks // 2).astype(jnp.int32)
        for head in range(heads):
            value = jnp.dot(
                slab_ref[0, head], up_ref[head], preferred_element_type=jnp.float32
            ).astype(jnp.bfloat16)
            rope = slab_ref[0, heads + head // 2]
            if head % 2:
                rope = jnp.concatenate([rope[:, LANES // 2 :], rope[:, : LANES // 2]], axis=-1)
            rows = pl.ds(head * half, half)
            out_ref[0, first, rows, :latent] = value[:half]
            out_ref[0, 1 - first, rows, :latent] = value[half:]
            out_ref[0, first, rows, latent:] = rope[:half]
            out_ref[0, 1 - first, rows, latent:] = rope[half:]

    return pl.pallas_call(
        kernel,
        out_shape=jax.ShapeDtypeStruct(
            (share, 2, heads * half, latent + LANES), jnp.bfloat16
        ),
        grid=(share,),
        in_specs=[
            SCALARS,
            SCALARS,
            pl.BlockSpec((1, n_slabs, tokens, LANES), lambda g: (g, 0, 0, 0)),
            pl.BlockSpec((heads, LANES, latent), lambda g: (0, 0, 0)),
        ],
        out_specs=pl.BlockSpec((1, 2, heads * half, latent + LANES), lambda g: (g, 0, 0, 0)),
        cost_estimate=cost(
            2 * share * heads * tokens * LANES * latent,
            share * heads * tokens * (latent + LANES) * 4,
        ),
        name="absorb",
    )(block_ids, place, slabs, key_up)


def attend(block_ids, place, query_full, keys, value_up, scale):
    share, _, rows, width = query_full.shape
    sources, tokens, _ = keys.shape
    heads, latent, value_dim = value_up.shape
    half = tokens // 2
    n_blocks = block_ids.shape[0]
    n_keys = sources * half
    factor = scale * LOG2_E

    def kernel(ids_ref, place_ref, query_ref, keys_ref, up_ref, out_ref, turned, plain, held, key_pos):
        step = pl.program_id(0)

        @pl.when(step == 0)
        def _():
            spot = lax.broadcasted_iota(jnp.int32, (8, n_keys), 1)
            low_pos = spot
            for source in range(sources):
                owner = place_ref[1] + source * place_ref[2]
                id_first = ids_ref[2 * owner]
                first = (id_first >= n_blocks // 2).astype(jnp.int32)
                low_id = jnp.minimum(id_first, n_blocks - 1 - id_first)
                low_pos = jnp.where(
                    spot // half == source, low_id * half + spot % half, low_pos
                )
                for side in range(2):
                    begin = jnp.where(first == side, 0, half)
                    begin = pl.multiple_of(begin, half)
                    plain[side, pl.ds(source * half, half), :] = keys_ref[
                        source, pl.ds(begin, half), :
                    ]
            key_pos[0] = low_pos
            low_block = low_pos // half
            key_pos[1] = (n_blocks - 1 - low_block) * half + low_pos % half
            for side in range(2):
                turned[side] = plain[side].T

        owner = place_ref[0] + step
        id_first = ids_ref[2 * owner]
        low_id = jnp.minimum(id_first, n_blocks - 1 - id_first)
        within = lax.broadcasted_iota(jnp.int32, (rows, 1), 0) % half

        def score(side, key_side):
            return (
                jnp.dot(query_ref[0, side], turned[key_side], preferred_element_type=jnp.float32)
                * factor
            )

        def masked(side, block):
            seen = key_pos[side, 0:1, :] <= block * half + within
            return seen, jnp.where(seen, score(side, side), LOW)

        lane = lax.broadcasted_iota(jnp.int32, (half, LANES), 1)

        def finish(side, top, total, weighted):
            some = total > 0.0
            safe = jnp.where(some, total, 1.0)
            value = (weighted * (1.0 / safe)).astype(jnp.bfloat16)
            level = jnp.where(some, top + jnp.log2(safe), LOW)
            high = level.astype(jnp.bfloat16).astype(jnp.float32)
            rest = level - high
            middle = rest.astype(jnp.bfloat16).astype(jnp.float32)
            parts = (high, middle, rest - middle)
            tile = jnp.zeros((half, LANES), jnp.float32)
            for head in range(heads):
                span = slice(head * half, (head + 1) * half)
                row = pl.multiple_of(step * tokens + side * half, half)
                held[head, pl.ds(row, half), :] = value[span]
                for at, part in enumerate(parts):
                    tile = jnp.where(lane == 3 * head + at, part[span], tile)
            out_ref[step, pl.ds(side * half, half), heads * value_dim :] = tile.astype(jnp.bfloat16)

        seen, low_low = masked(0, low_id)
        top = jnp.max(low_low, axis=1, keepdims=True)
        expo = jnp.where(seen, jnp.exp2(low_low - top), 0.0)
        total = jnp.sum(expo, axis=1, keepdims=True)
        weighted = jnp.dot(
            expo.astype(jnp.bfloat16), plain[0, :, :latent], preferred_element_type=jnp.float32
        )
        finish(0, top, total, weighted)

        high_low = score(1, 0)
        seen, high_high = masked(1, n_blocks - 1 - low_id)
        top = jnp.maximum(
            jnp.max(high_low, axis=1, keepdims=True), jnp.max(high_high, axis=1, keepdims=True)
        )
        expo_low = jnp.exp2(high_low - top)
        expo_high = jnp.where(seen, jnp.exp2(high_high - top), 0.0)
        total = jnp.sum(expo_low, axis=1, keepdims=True) + jnp.sum(
            expo_high, axis=1, keepdims=True
        )
        weighted = jnp.dot(
            expo_low.astype(jnp.bfloat16), plain[0, :, :latent], preferred_element_type=jnp.float32
        ) + jnp.dot(
            expo_high.astype(jnp.bfloat16), plain[1, :, :latent], preferred_element_type=jnp.float32
        )
        finish(1, top, total, weighted)

        @pl.when(step == share - 1)
        def _():
            for head in range(heads):
                value = jnp.dot(held[head], up_ref[head], preferred_element_type=jnp.float32)
                out_ref[:, :, head * value_dim : (head + 1) * value_dim] = value.astype(
                    jnp.bfloat16
                ).reshape(share, tokens, value_dim)

    out_width = heads * value_dim + LANES
    return pl.pallas_call(
        kernel,
        out_shape=jax.ShapeDtypeStruct((share, tokens, out_width), jnp.bfloat16),
        grid=(share,),
        in_specs=[
            SCALARS,
            SCALARS,
            pl.BlockSpec((1, 2, rows, width), lambda g: (g, 0, 0, 0)),
            pl.BlockSpec((sources, tokens, width), lambda g: (0, 0, 0)),
            pl.BlockSpec((heads, latent, value_dim), lambda g: (0, 0, 0)),
        ],
        out_specs=pl.BlockSpec((share, tokens, out_width), lambda g: (0, 0, 0)),
        scratch_shapes=[
            pltpu.VMEM((2, width, n_keys), jnp.bfloat16),
            pltpu.VMEM((2, n_keys, width), jnp.bfloat16),
            pltpu.VMEM((heads, share * tokens, latent), jnp.bfloat16),
            pltpu.VMEM((2, 8, n_keys), jnp.int32),
        ],
        cost_estimate=cost(
            share * 6 * rows * n_keys * (width + latent), share * rows * width * 4
        ),
        name="attend",
    )(block_ids, place, query_full, keys, value_up)


def combine(block_ids, place, parts, heads):
    share, tokens, width = parts.shape
    value_width = width - LANES
    value_dim = value_width // heads
    half = tokens // 2
    n_blocks = block_ids.shape[0]

    def kernel(ids_ref, place_ref, parts_ref, out_ref):
        first = (ids_ref[2 * place_ref[3]] >= n_blocks // 2).astype(jnp.int32)
        for side in range(2):
            begin = pl.multiple_of(jnp.where(first == side, 0, half), half)
            span = slice(side * half, (side + 1) * half)
            stats = [parts_ref[k, span, value_width:].astype(jnp.float32) for k in range(share)]
            for head in range(heads):
                levels = [
                    s[:, 3 * head : 3 * head + 1]
                    + s[:, 3 * head + 1 : 3 * head + 2]
                    + s[:, 3 * head + 2 : 3 * head + 3]
                    for s in stats
                ]
                top = functools.reduce(jnp.maximum, levels)
                shares = [jnp.exp2(level - top) for level in levels]
                inverse = 1.0 / functools.reduce(jnp.add, shares)
                columns = slice(head * value_dim, (head + 1) * value_dim)
                value = jnp.zeros((half, value_dim), jnp.float32)
                for k in range(share):
                    value += parts_ref[k, span, columns].astype(jnp.float32) * (
                        shares[k] * inverse
                    )
                out_ref[0, pl.ds(begin, half), columns] = value.astype(jnp.bfloat16)

    return pl.pallas_call(
        kernel,
        out_shape=jax.ShapeDtypeStruct((1, tokens, value_width), jnp.bfloat16),
        in_specs=[SCALARS, SCALARS, WHOLE],
        out_specs=WHOLE,
        cost_estimate=cost(0, share * tokens * width * 2),
        name="combine",
    )(block_ids, place, parts)


def shards(outgoing, w_down, kv_gain, queries, w_key_up, w_value_up, block_ids):
    section_idx = lax.axis_index("pp")
    n_y0, n_x, tp_size = (lax.axis_size(a) for a in ("y0", "x", "tp"))
    n_share = n_y0 * n_x
    n_keys = lax.axis_size("y1")
    tokens, heads, query_dim = queries.shape[1:]
    y1, y0, x = (lax.axis_index(a).astype(jnp.int32) for a in CTX)
    column = y0 * n_x + x
    place = jnp.stack([y1 * n_share, column, jnp.int32(n_share), y1 * n_share + column])

    slabs = pack_queries(queries[0], n_share)
    moved = lax.ppermute(outgoing, "pp", [(0, 1)])
    section_in = jnp.where(section_idx == 0, outgoing, moved)[0]
    with jax.named_scope("share"):
        shared = exchange(slabs, SHARE)
    partial_value = jnp.dot(section_in, w_down[0], preferred_element_type=jnp.float32)
    with jax.named_scope("reduce"):
        pieces = exchange(partial_value.reshape(tp_size, tokens // tp_size, -1), ("tp",))
    local = norm_rows(pieces, kv_gain, tp_size)
    with jax.named_scope("spread"):
        key_rows = exchange(local, ("tp",)).reshape(tokens, -1)
    with jax.named_scope("keys"):
        keys = exchange(jnp.broadcast_to(key_rows, (n_keys, *key_rows.shape)), KEYS)

    query_full = absorb(block_ids, place, shared, w_key_up[0])
    part_out = attend(block_ids, place, query_full, keys, w_value_up[0], query_dim**-0.5)
    with jax.named_scope("parts"):
        got = exchange(part_out, SHARE)
    return combine(block_ids, place, got, heads)


def build(torus):
    placed = (
        P("pp", CTX, "tp"),
        P("pp", "tp", None),
        P("pp", None),
        P("pp", CTX, "tp", None),
        P("pp", "tp", None, None),
        P("pp", "tp", None, None),
        P(),
    )
    return jax.shard_map(
        shards, mesh=torus, in_specs=placed, out_specs=P("pp", CTX, "tp"), check_vma=False
    )


def solution(mesh):
    torus = Mesh(
        mesh.devices.reshape(4, 2, 4, mesh.shape["pp"], mesh.shape["tp"]),
        ("y1", "y0", "x", "pp", "tp"),
    )
    return build(torus)
```

```python
import functools

import jax
import jax.numpy as jnp
from jax import lax
from jax.experimental import pallas as pl
from jax.experimental.pallas import tpu as pltpu
from jax.sharding import Mesh
from jax.sharding import PartitionSpec as P

CTX = ("y", "x")
SHARE = "x"
KEYS = "y"
LANES = 128
LOG2_E = 1.4426950408889634
LOW = -1e30
WHOLE = pl.BlockSpec(memory_space=pltpu.VMEM)
SCALARS = pl.BlockSpec(memory_space=pltpu.SMEM)


def exchange(array, axes):
    return lax.all_to_all(array, axes, 0, 0, tiled=True)


def cost(flops, bytes_accessed):
    return pl.CostEstimate(flops=flops, bytes_accessed=bytes_accessed, transcendentals=0)


def pack_queries(query):
    tokens, heads, width = query.shape
    nope = LANES
    rope = width - nope
    slabs = heads + heads * rope // LANES

    def kernel(query_ref, out_ref):
        rows = query_ref[...]
        for head in range(heads):
            out_ref[head] = rows[:, head, :nope]
        for pair in range(heads // 2):
            out_ref[heads + pair] = jnp.concatenate(
                [rows[:, 2 * pair, nope:], rows[:, 2 * pair + 1, nope:]], axis=-1
            )

    return pl.pallas_call(
        kernel,
        out_shape=jax.ShapeDtypeStruct((slabs, tokens, LANES), query.dtype),
        in_specs=[WHOLE],
        out_specs=WHOLE,
        cost_estimate=cost(0, 2 * slabs * tokens * LANES * 2),
        name="pack_queries",
    )(query)


def project(section_in, w_down, pieces):
    tokens, depth = section_in.shape
    width = w_down.shape[-1]
    padded = -(-width // LANES) * LANES
    rows = tokens // pieces

    def kernel(in_ref, down_ref, out_ref):
        value = jnp.dot(in_ref[...], down_ref[...], preferred_element_type=jnp.float32)
        out_ref[:, :, :width] = value.reshape(pieces, rows, width)
        out_ref[:, :, width:] = jnp.zeros((pieces, rows, padded - width), jnp.float32)

    return pl.pallas_call(
        kernel,
        out_shape=jax.ShapeDtypeStruct((pieces, rows, padded), jnp.float32),
        in_specs=[WHOLE, WHOLE],
        out_specs=WHOLE,
        cost_estimate=cost(2 * tokens * depth * width, tokens * padded * 4),
        name="project",
    )(section_in, w_down)


def norm_rows(pieces, gain, copies):
    parts, rows, width = pieces.shape
    latent = gain.shape[-1]

    def kernel(pieces_ref, gain_ref, out_ref):
        raw = pieces_ref[0]
        for part in range(1, parts):
            raw = raw + pieces_ref[part]
        latent_part = raw[:, :latent]
        mean_sq = jnp.mean(latent_part * latent_part, axis=-1, keepdims=True)
        normed = latent_part * lax.rsqrt(mean_sq + 1e-06) * gain_ref[...]
        row = jnp.concatenate([normed, raw[:, latent:]], axis=-1).astype(jnp.bfloat16)
        for copy in range(copies):
            out_ref[copy] = row

    return pl.pallas_call(
        kernel,
        out_shape=jax.ShapeDtypeStruct((copies, rows, latent + LANES), jnp.bfloat16),
        in_specs=[WHOLE, WHOLE],
        out_specs=WHOLE,
        cost_estimate=cost(0, parts * rows * width * 8),
        name="norm_rows",
    )(pieces, gain)


def absorb(block_ids, place, slabs, key_up):
    share = len(slabs)
    _, tokens, _ = slabs[0].shape
    heads, _, latent = key_up.shape
    half = tokens // 2
    n_blocks = block_ids.shape[0]

    def kernel(ids_ref, place_ref, *refs):
        slab_refs, up_ref, out_ref = refs[:share], refs[share], refs[share + 1]
        for back, slab_ref in enumerate(slab_refs):
            owner = place_ref[0] + lax.rem(place_ref[1] + share - back, share)
            first = (ids_ref[2 * owner] >= n_blocks // 2).astype(jnp.int32)
            for head in range(heads):
                value = jnp.dot(
                    slab_ref[head], up_ref[head], preferred_element_type=jnp.float32
                ).astype(jnp.bfloat16)
                rope = slab_ref[heads + head // 2]
                if head % 2:
                    rope = jnp.concatenate(
                        [rope[:, LANES // 2 :], rope[:, : LANES // 2]], axis=-1
                    )
                rows = pl.ds(head * half, half)
                out_ref[back, first, rows, :latent] = value[:half]
                out_ref[back, 1 - first, rows, :latent] = value[half:]
                out_ref[back, first, rows, latent:] = rope[:half]
                out_ref[back, 1 - first, rows, latent:] = rope[half:]

    return pl.pallas_call(
        kernel,
        out_shape=jax.ShapeDtypeStruct(
            (share, 2, heads * half, latent + LANES), jnp.bfloat16
        ),
        in_specs=[SCALARS, SCALARS] + [WHOLE] * (share + 1),
        out_specs=WHOLE,
        cost_estimate=cost(
            2 * share * heads * tokens * LANES * latent,
            share * heads * tokens * (latent + LANES) * 4,
        ),
        name="absorb",
    )(block_ids, place, *slabs, key_up)


def attend(block_ids, place, query_full, keys, value_up, scale):
    share, _, rows, width = query_full.shape
    sources, tokens, _ = keys.shape
    heads, latent, value_dim = value_up.shape
    half = tokens // 2
    n_blocks = block_ids.shape[0]
    n_keys = sources * half
    factor = scale * LOG2_E

    def kernel(ids_ref, place_ref, query_ref, keys_ref, up_ref, out_ref, turned, plain, held, key_pos):
        step = pl.program_id(0)

        @pl.when(step == 0)
        def _():
            spot = lax.broadcasted_iota(jnp.int32, (8, n_keys), 1)
            low_pos = spot
            for source in range(sources):
                owner = place_ref[1] + source * place_ref[2]
                id_first = ids_ref[2 * owner]
                first = (id_first >= n_blocks // 2).astype(jnp.int32)
                low_id = jnp.minimum(id_first, n_blocks - 1 - id_first)
                low_pos = jnp.where(
                    spot // half == source, low_id * half + spot % half, low_pos
                )
                for side in range(2):
                    begin = jnp.where(first == side, 0, half)
                    begin = pl.multiple_of(begin, half)
                    plain[side, pl.ds(source * half, half), :] = keys_ref[
                        source, pl.ds(begin, half), :
                    ]
            key_pos[0] = low_pos
            low_block = low_pos // half
            key_pos[1] = (n_blocks - 1 - low_block) * half + low_pos % half
            for side in range(2):
                turned[side] = plain[side].T

        receiver = lax.rem(place_ref[1] + share - step, share)
        id_first = ids_ref[2 * (place_ref[0] + receiver)]
        low_id = jnp.minimum(id_first, n_blocks - 1 - id_first)
        within = lax.broadcasted_iota(jnp.int32, (rows, 1), 0) % half

        def score(side, key_side):
            return (
                jnp.dot(query_ref[0, side], turned[key_side], preferred_element_type=jnp.float32)
                * factor
            )

        def masked(side, block):
            seen = key_pos[side, 0:1, :] <= block * half + within
            return seen, jnp.where(seen, score(side, side), LOW)

        lane = lax.broadcasted_iota(jnp.int32, (half, LANES), 1)

        def finish(side, top, total, weighted):
            some = total > 0.0
            safe = jnp.where(some, total, 1.0)
            value = (weighted * (1.0 / safe)).astype(jnp.bfloat16)
            level = jnp.where(some, top + jnp.log2(safe), LOW)
            high = level.astype(jnp.bfloat16).astype(jnp.float32)
            rest = level - high
            middle = rest.astype(jnp.bfloat16).astype(jnp.float32)
            parts = (high, middle, rest - middle)
            tile = jnp.zeros((half, LANES), jnp.float32)
            for head in range(heads):
                span = slice(head * half, (head + 1) * half)
                row = pl.multiple_of(receiver * tokens + side * half, half)
                held[head, pl.ds(row, half), :] = value[span]
                for at, part in enumerate(parts):
                    tile = jnp.where(lane == 3 * head + at, part[span], tile)
            out_ref[receiver, pl.ds(side * half, half), heads * value_dim :] = tile.astype(jnp.bfloat16)

        seen, low_low = masked(0, low_id)
        top = jnp.max(low_low, axis=1, keepdims=True)
        expo = jnp.where(seen, jnp.exp2(low_low - top), 0.0)
        total = jnp.sum(expo, axis=1, keepdims=True)
        weighted = jnp.dot(
            expo.astype(jnp.bfloat16), plain[0, :, :latent], preferred_element_type=jnp.float32
        )
        finish(0, top, total, weighted)

        high_low = score(1, 0)
        seen, high_high = masked(1, n_blocks - 1 - low_id)
        top = jnp.maximum(
            jnp.max(high_low, axis=1, keepdims=True), jnp.max(high_high, axis=1, keepdims=True)
        )
        expo_low = jnp.exp2(high_low - top)
        expo_high = jnp.where(seen, jnp.exp2(high_high - top), 0.0)
        total = jnp.sum(expo_low, axis=1, keepdims=True) + jnp.sum(
            expo_high, axis=1, keepdims=True
        )
        weighted = jnp.dot(
            expo_low.astype(jnp.bfloat16), plain[0, :, :latent], preferred_element_type=jnp.float32
        ) + jnp.dot(
            expo_high.astype(jnp.bfloat16), plain[1, :, :latent], preferred_element_type=jnp.float32
        )
        finish(1, top, total, weighted)

        @pl.when(step == share - 1)
        def _():
            for head in range(heads):
                value = jnp.dot(held[head], up_ref[head], preferred_element_type=jnp.float32)
                out_ref[:, :, head * value_dim : (head + 1) * value_dim] = value.astype(
                    jnp.bfloat16
                ).reshape(share, tokens, value_dim)

    out_width = heads * value_dim + LANES
    return pl.pallas_call(
        kernel,
        out_shape=jax.ShapeDtypeStruct((share, tokens, out_width), jnp.bfloat16),
        grid=(share,),
        in_specs=[
            SCALARS,
            SCALARS,
            pl.BlockSpec((1, 2, rows, width), lambda g: (g, 0, 0, 0)),
            pl.BlockSpec((sources, tokens, width), lambda g: (0, 0, 0)),
            pl.BlockSpec((heads, latent, value_dim), lambda g: (0, 0, 0)),
        ],
        out_specs=pl.BlockSpec((share, tokens, out_width), lambda g: (0, 0, 0)),
        scratch_shapes=[
            pltpu.VMEM((2, width, n_keys), jnp.bfloat16),
            pltpu.VMEM((2, n_keys, width), jnp.bfloat16),
            pltpu.VMEM((heads, share * tokens, latent), jnp.bfloat16),
            pltpu.VMEM((2, 8, n_keys), jnp.int32),
        ],
        cost_estimate=cost(
            share * 6 * rows * n_keys * (width + latent), share * rows * width * 4
        ),
        name="attend",
    )(block_ids, place, query_full, keys, value_up)


def combine(block_ids, place, parts, heads):
    share, tokens, width = parts.shape
    value_width = width - LANES
    value_dim = value_width // heads
    half = tokens // 2
    n_blocks = block_ids.shape[0]

    def kernel(ids_ref, place_ref, parts_ref, out_ref):
        first = (ids_ref[2 * (place_ref[0] + place_ref[1])] >= n_blocks // 2).astype(jnp.int32)
        for side in range(2):
            begin = pl.multiple_of(jnp.where(first == side, 0, half), half)
            span = slice(side * half, (side + 1) * half)
            stats = [parts_ref[k, span, value_width:].astype(jnp.float32) for k in range(share)]
            for head in range(heads):
                levels = [
                    s[:, 3 * head : 3 * head + 1]
                    + s[:, 3 * head + 1 : 3 * head + 2]
                    + s[:, 3 * head + 2 : 3 * head + 3]
                    for s in stats
                ]
                top = functools.reduce(jnp.maximum, levels)
                shares = [jnp.exp2(level - top) for level in levels]
                inverse = 1.0 / functools.reduce(jnp.add, shares)
                columns = slice(head * value_dim, (head + 1) * value_dim)
                value = jnp.zeros((half, value_dim), jnp.float32)
                for k in range(share):
                    value += parts_ref[k, span, columns].astype(jnp.float32) * (
                        shares[k] * inverse
                    )
                out_ref[0, pl.ds(begin, half), columns] = value.astype(jnp.bfloat16)

    return pl.pallas_call(
        kernel,
        out_shape=jax.ShapeDtypeStruct((1, tokens, value_width), jnp.bfloat16),
        in_specs=[SCALARS, SCALARS, WHOLE],
        out_specs=WHOLE,
        cost_estimate=cost(0, share * tokens * width * 2),
        name="combine",
    )(block_ids, place, parts)


def shards(outgoing, w_down, kv_gain, queries, w_key_up, w_value_up, block_ids):
    section_idx = lax.axis_index("pp")
    n_share, n_keys, tp_size = (lax.axis_size(a) for a in (SHARE, KEYS, "tp"))
    tokens, heads, query_dim = queries.shape[1:]
    y, x = (lax.axis_index(a).astype(jnp.int32) for a in CTX)
    place = jnp.stack([y * n_share, x, jnp.int32(n_share)])

    moved = lax.ppermute(outgoing, "pp", [(0, 1)])
    section_in = jnp.where(section_idx == 0, outgoing, moved)[0]
    partial_value = project(section_in, w_down[0], tp_size)
    pieces = exchange(partial_value, ("tp",))
    slabs = [pack_queries(queries[0])]
    for ahead in range(1, n_share):
        pairs = [(i, (i + ahead) % n_share) for i in range(n_share)]
        slabs.append(lax.ppermute(slabs[0], SHARE, pairs))
    local = norm_rows(pieces, kv_gain, tp_size)
    key_rows = exchange(local, ("tp",)).reshape(tokens, -1)
    query_full = absorb(block_ids, place, slabs, w_key_up[0])
    keys = exchange(jnp.broadcast_to(key_rows, (n_keys, *key_rows.shape)), (KEYS,))
    part_out = attend(block_ids, place, query_full, keys, w_value_up[0], query_dim**-0.5)
    got = exchange(part_out, (SHARE,))
    return combine(block_ids, place, got, heads)


def build(torus):
    placed = (
        P("pp", CTX, "tp"),
        P("pp", "tp", None),
        P("pp", None),
        P("pp", CTX, "tp", None),
        P("pp", "tp", None, None),
        P("pp", "tp", None, None),
        P(),
    )
    return jax.shard_map(
        shards, mesh=torus, in_specs=placed, out_specs=P("pp", CTX, "tp"), check_vma=False
    )


def solution(mesh):
    torus = Mesh(
        mesh.devices.reshape(8, 4, mesh.shape["pp"], mesh.shape["tp"]),
        ("y", "x", "pp", "tp"),
    )
    return build(torus)
```

```python
import functools

import jax
import jax.numpy as jnp
from jax import lax
from jax.experimental import pallas as pl
from jax.experimental.pallas import tpu as pltpu
from jax.sharding import Mesh
from jax.sharding import PartitionSpec as P

CTX = ("y", "x")
SHARE = "x"
KEYS = "y"
LANES = 128
LOG2_E = 1.4426950408889634
LOW = -1e30
MIB = 1 << 20
WHOLE = pl.BlockSpec(memory_space=pltpu.VMEM)
SCALARS = pl.BlockSpec(memory_space=pltpu.SMEM)


def exchange(array, axes):
    return lax.all_to_all(array, axes, 0, 0, tiled=True)


def cost(flops, bytes_accessed):
    return pl.CostEstimate(flops=flops, bytes_accessed=bytes_accessed, transcendentals=0)


def pack_queries(query):
    tokens, heads, width = query.shape
    nope = LANES
    rope = width - nope
    slabs = heads + heads * rope // LANES

    def kernel(query_ref, out_ref):
        rows = query_ref[...]
        for head in range(heads):
            out_ref[head] = rows[:, head, :nope]
        for pair in range(heads // 2):
            out_ref[heads + pair] = jnp.concatenate(
                [rows[:, 2 * pair, nope:], rows[:, 2 * pair + 1, nope:]], axis=-1
            )

    return pl.pallas_call(
        kernel,
        out_shape=jax.ShapeDtypeStruct((slabs, tokens, LANES), query.dtype),
        in_specs=[WHOLE],
        out_specs=WHOLE,
        cost_estimate=cost(0, 2 * slabs * tokens * LANES * 2),
        compiler_params=pltpu.CompilerParams(vmem_limit_bytes=4 * MIB),
        name="pack_queries",
    )(query)


def project(section_in, w_down, pieces):
    tokens, depth = section_in.shape
    width = w_down.shape[-1]
    padded = -(-width // LANES) * LANES
    rows = tokens // pieces

    def kernel(in_ref, down_ref, out_ref):
        value = jnp.dot(in_ref[...], down_ref[...], preferred_element_type=jnp.float32)
        out_ref[:, :, :width] = value.reshape(pieces, rows, width)
        out_ref[:, :, width:] = jnp.zeros((pieces, rows, padded - width), jnp.float32)

    return pl.pallas_call(
        kernel,
        out_shape=jax.ShapeDtypeStruct((pieces, rows, padded), jnp.float32),
        in_specs=[WHOLE, WHOLE],
        out_specs=WHOLE,
        cost_estimate=cost(2 * tokens * depth * width, tokens * padded * 4),
        compiler_params=pltpu.CompilerParams(vmem_limit_bytes=6 * MIB),
        name="project",
    )(section_in, w_down)


def norm_rows(pieces, gain, copies):
    parts, rows, width = pieces.shape
    latent = gain.shape[-1]

    def kernel(pieces_ref, gain_ref, out_ref):
        raw = pieces_ref[0]
        for part in range(1, parts):
            raw = raw + pieces_ref[part]
        latent_part = raw[:, :latent]
        mean_sq = jnp.mean(latent_part * latent_part, axis=-1, keepdims=True)
        normed = latent_part * lax.rsqrt(mean_sq + 1e-06) * gain_ref[...]
        row = jnp.concatenate([normed, raw[:, latent:]], axis=-1).astype(jnp.bfloat16)
        for copy in range(copies):
            out_ref[copy] = row

    return pl.pallas_call(
        kernel,
        out_shape=jax.ShapeDtypeStruct((copies, rows, latent + LANES), jnp.bfloat16),
        in_specs=[WHOLE, WHOLE],
        out_specs=WHOLE,
        cost_estimate=cost(0, parts * rows * width * 8),
        compiler_params=pltpu.CompilerParams(vmem_limit_bytes=4 * MIB),
        name="norm_rows",
    )(pieces, gain)


def absorb(block_ids, place, slabs, key_up):
    share = len(slabs)
    _, tokens, _ = slabs[0].shape
    heads, _, latent = key_up.shape
    half = tokens // 2
    n_blocks = block_ids.shape[0]

    def kernel(ids_ref, place_ref, *refs):
        slab_refs, up_ref, out_ref = refs[:share], refs[share], refs[share + 1]
        for back, slab_ref in enumerate(slab_refs):
            owner = place_ref[0] + lax.rem(place_ref[1] + share - back, share)
            first = (ids_ref[2 * owner] >= n_blocks // 2).astype(jnp.int32)
            for head in range(heads):
                value = jnp.dot(
                    slab_ref[head], up_ref[head], preferred_element_type=jnp.float32
                ).astype(jnp.bfloat16)
                rope = slab_ref[heads + head // 2]
                if head % 2:
                    rope = jnp.concatenate(
                        [rope[:, LANES // 2 :], rope[:, : LANES // 2]], axis=-1
                    )
                rows = pl.ds(head * half, half)
                out_ref[back, first, rows, :latent] = value[:half]
                out_ref[back, 1 - first, rows, :latent] = value[half:]
                out_ref[back, first, rows, latent:] = rope[:half]
                out_ref[back, 1 - first, rows, latent:] = rope[half:]

    return pl.pallas_call(
        kernel,
        out_shape=jax.ShapeDtypeStruct(
            (share, 2, heads * half, latent + LANES), jnp.bfloat16
        ),
        in_specs=[SCALARS, SCALARS] + [WHOLE] * (share + 1),
        out_specs=WHOLE,
        cost_estimate=cost(
            2 * share * heads * tokens * LANES * latent,
            share * heads * tokens * (latent + LANES) * 4,
        ),
        compiler_params=pltpu.CompilerParams(vmem_limit_bytes=6 * MIB),
        name="absorb",
    )(block_ids, place, *slabs, key_up)


def attend(block_ids, place, query_full, keys, value_up, scale):
    share, _, rows, width = query_full.shape
    sources, tokens, _ = keys.shape
    heads, latent, value_dim = value_up.shape
    half = tokens // 2
    n_blocks = block_ids.shape[0]
    n_keys = sources * half
    factor = scale * LOG2_E

    def kernel(ids_ref, place_ref, query_ref, keys_ref, up_ref, out_ref, turned, plain, held, key_pos):
        step = pl.program_id(0)

        @pl.when(step == 0)
        def _():
            spot = lax.broadcasted_iota(jnp.int32, (8, n_keys), 1)
            low_pos = spot
            for source in range(sources):
                owner = place_ref[1] + source * place_ref[2]
                id_first = ids_ref[2 * owner]
                first = (id_first >= n_blocks // 2).astype(jnp.int32)
                low_id = jnp.minimum(id_first, n_blocks - 1 - id_first)
                low_pos = jnp.where(
                    spot // half == source, low_id * half + spot % half, low_pos
                )
                for side in range(2):
                    begin = jnp.where(first == side, 0, half)
                    begin = pl.multiple_of(begin, half)
                    plain[side, pl.ds(source * half, half), :] = keys_ref[
                        source, pl.ds(begin, half), :
                    ]
            key_pos[0] = low_pos
            low_block = low_pos // half
            key_pos[1] = (n_blocks - 1 - low_block) * half + low_pos % half
            for side in range(2):
                turned[side] = plain[side].T

        receiver = lax.rem(place_ref[1] + share - step, share)
        id_first = ids_ref[2 * (place_ref[0] + receiver)]
        low_id = jnp.minimum(id_first, n_blocks - 1 - id_first)
        within = lax.broadcasted_iota(jnp.int32, (rows, 1), 0) % half

        def score(side, key_side):
            return (
                jnp.dot(query_ref[0, side], turned[key_side], preferred_element_type=jnp.float32)
                * factor
            )

        def masked(side, block):
            seen = key_pos[side, 0:1, :] <= block * half + within
            return seen, jnp.where(seen, score(side, side), LOW)

        lane = lax.broadcasted_iota(jnp.int32, (half, LANES), 1)

        def finish(side, top, total, weighted):
            some = total > 0.0
            safe = jnp.where(some, total, 1.0)
            value = (weighted * (1.0 / safe)).astype(jnp.bfloat16)
            level = jnp.where(some, top + jnp.log2(safe), LOW)
            high = level.astype(jnp.bfloat16).astype(jnp.float32)
            rest = level - high
            middle = rest.astype(jnp.bfloat16).astype(jnp.float32)
            parts = (high, middle, rest - middle)
            tile = jnp.zeros((half, LANES), jnp.float32)
            for head in range(heads):
                span = slice(head * half, (head + 1) * half)
                row = pl.multiple_of(receiver * tokens + side * half, half)
                held[head, pl.ds(row, half), :] = value[span]
                for at, part in enumerate(parts):
                    tile = jnp.where(lane == 3 * head + at, part[span], tile)
            out_ref[receiver, pl.ds(side * half, half), heads * value_dim :] = tile.astype(jnp.bfloat16)

        seen, low_low = masked(0, low_id)
        top = jnp.max(low_low, axis=1, keepdims=True)
        expo = jnp.where(seen, jnp.exp2(low_low - top), 0.0)
        total = jnp.sum(expo, axis=1, keepdims=True)
        weighted = jnp.dot(
            expo.astype(jnp.bfloat16), plain[0, :, :latent], preferred_element_type=jnp.float32
        )
        finish(0, top, total, weighted)

        high_low = score(1, 0)
        seen, high_high = masked(1, n_blocks - 1 - low_id)
        top = jnp.maximum(
            jnp.max(high_low, axis=1, keepdims=True), jnp.max(high_high, axis=1, keepdims=True)
        )
        expo_low = jnp.exp2(high_low - top)
        expo_high = jnp.where(seen, jnp.exp2(high_high - top), 0.0)
        total = jnp.sum(expo_low, axis=1, keepdims=True) + jnp.sum(
            expo_high, axis=1, keepdims=True
        )
        weighted = jnp.dot(
            expo_low.astype(jnp.bfloat16), plain[0, :, :latent], preferred_element_type=jnp.float32
        ) + jnp.dot(
            expo_high.astype(jnp.bfloat16), plain[1, :, :latent], preferred_element_type=jnp.float32
        )
        finish(1, top, total, weighted)

        @pl.when(step == share - 1)
        def _():
            for head in range(heads):
                value = jnp.dot(held[head], up_ref[head], preferred_element_type=jnp.float32)
                out_ref[:, :, head * value_dim : (head + 1) * value_dim] = value.astype(
                    jnp.bfloat16
                ).reshape(share, tokens, value_dim)

    out_width = heads * value_dim + LANES
    return pl.pallas_call(
        kernel,
        out_shape=jax.ShapeDtypeStruct((share, tokens, out_width), jnp.bfloat16),
        grid=(share,),
        in_specs=[
            SCALARS,
            SCALARS,
            pl.BlockSpec((1, 2, rows, width), lambda g: (g, 0, 0, 0)),
            pl.BlockSpec((sources, tokens, width), lambda g: (0, 0, 0)),
            pl.BlockSpec((heads, latent, value_dim), lambda g: (0, 0, 0)),
        ],
        out_specs=pl.BlockSpec((share, tokens, out_width), lambda g: (0, 0, 0)),
        scratch_shapes=[
            pltpu.VMEM((2, width, n_keys), jnp.bfloat16),
            pltpu.VMEM((2, n_keys, width), jnp.bfloat16),
            pltpu.VMEM((heads, share * tokens, latent), jnp.bfloat16),
            pltpu.VMEM((2, 8, n_keys), jnp.int32),
        ],
        cost_estimate=cost(
            share * 6 * rows * n_keys * (width + latent), share * rows * width * 4
        ),
        compiler_params=pltpu.CompilerParams(vmem_limit_bytes=24 * MIB),
        name="attend",
    )(block_ids, place, query_full, keys, value_up)


def combine(block_ids, place, parts, heads):
    share, tokens, width = parts.shape
    value_width = width - LANES
    value_dim = value_width // heads
    half = tokens // 2
    n_blocks = block_ids.shape[0]

    def kernel(ids_ref, place_ref, parts_ref, out_ref):
        first = (ids_ref[2 * (place_ref[0] + place_ref[1])] >= n_blocks // 2).astype(jnp.int32)
        for side in range(2):
            begin = pl.multiple_of(jnp.where(first == side, 0, half), half)
            span = slice(side * half, (side + 1) * half)
            stats = [parts_ref[k, span, value_width:].astype(jnp.float32) for k in range(share)]
            for head in range(heads):
                levels = [
                    s[:, 3 * head : 3 * head + 1]
                    + s[:, 3 * head + 1 : 3 * head + 2]
                    + s[:, 3 * head + 2 : 3 * head + 3]
                    for s in stats
                ]
                top = functools.reduce(jnp.maximum, levels)
                shares = [jnp.exp2(level - top) for level in levels]
                inverse = 1.0 / functools.reduce(jnp.add, shares)
                columns = slice(head * value_dim, (head + 1) * value_dim)
                value = jnp.zeros((half, value_dim), jnp.float32)
                for k in range(share):
                    value += parts_ref[k, span, columns].astype(jnp.float32) * (
                        shares[k] * inverse
                    )
                out_ref[0, pl.ds(begin, half), columns] = value.astype(jnp.bfloat16)

    return pl.pallas_call(
        kernel,
        out_shape=jax.ShapeDtypeStruct((1, tokens, value_width), jnp.bfloat16),
        in_specs=[SCALARS, SCALARS, WHOLE],
        out_specs=WHOLE,
        cost_estimate=cost(0, share * tokens * width * 2),
        compiler_params=pltpu.CompilerParams(vmem_limit_bytes=6 * MIB),
        name="combine",
    )(block_ids, place, parts)


def shards(outgoing, w_down, kv_gain, queries, w_key_up, w_value_up, block_ids):
    section_idx = lax.axis_index("pp")
    n_share, n_keys, tp_size = (lax.axis_size(a) for a in (SHARE, KEYS, "tp"))
    tokens, heads, query_dim = queries.shape[1:]
    y, x = (lax.axis_index(a).astype(jnp.int32) for a in CTX)
    place = jnp.stack([y * n_share, x, jnp.int32(n_share)])

    moved = lax.ppermute(outgoing, "pp", [(0, 1)])
    section_in = jnp.where(section_idx == 0, outgoing, moved)[0]
    partial_value = project(section_in, w_down[0], tp_size)
    pieces = exchange(partial_value, ("tp",))
    slabs = [pack_queries(queries[0])]
    for ahead in range(1, n_share):
        pairs = [(i, (i + ahead) % n_share) for i in range(n_share)]
        slabs.append(lax.ppermute(slabs[0], SHARE, pairs))
    local = norm_rows(pieces, kv_gain, tp_size)
    key_rows = exchange(local, ("tp",)).reshape(tokens, -1)
    query_full = absorb(block_ids, place, slabs, w_key_up[0])
    keys = exchange(jnp.broadcast_to(key_rows, (n_keys, *key_rows.shape)), (KEYS,))
    part_out = attend(block_ids, place, query_full, keys, w_value_up[0], query_dim**-0.5)
    got = exchange(part_out, (SHARE,))
    return combine(block_ids, place, got, heads)


def build(torus):
    placed = (
        P("pp", CTX, "tp"),
        P("pp", "tp", None),
        P("pp", None),
        P("pp", CTX, "tp", None),
        P("pp", "tp", None, None),
        P("pp", "tp", None, None),
        P(),
    )
    return jax.shard_map(
        shards, mesh=torus, in_specs=placed, out_specs=P("pp", CTX, "tp"), check_vma=False
    )


def solution(mesh):
    torus = Mesh(
        mesh.devices.reshape(8, 4, mesh.shape["pp"], mesh.shape["tp"]),
        ("y", "x", "pp", "tp"),
    )
    return build(torus)
```

```python
import functools

import jax
import jax.numpy as jnp
from jax import lax
from jax.experimental import pallas as pl
from jax.experimental.pallas import tpu as pltpu
from jax.sharding import Mesh
from jax.sharding import PartitionSpec as P

CTX = ("y1", "y0", "x")
SHARE = "y1"
KEYS = ("y0", "x")
LANES = 128
LOG2_E = 1.4426950408889634
LOW = -1e30
MIB = 1 << 20
WHOLE = pl.BlockSpec(memory_space=pltpu.VMEM)
SCALARS = pl.BlockSpec(memory_space=pltpu.SMEM)


def exchange(array, axes):
    return lax.all_to_all(array, axes, 0, 0, tiled=True)


def cost(flops, bytes_accessed):
    return pl.CostEstimate(flops=flops, bytes_accessed=bytes_accessed, transcendentals=0)


def pack_queries(query):
    tokens, heads, width = query.shape
    nope = LANES
    rope = width - nope
    slabs = heads + heads * rope // LANES

    def kernel(query_ref, out_ref):
        rows = query_ref[...]
        for head in range(heads):
            out_ref[head] = rows[:, head, :nope]
        for pair in range(heads // 2):
            out_ref[heads + pair] = jnp.concatenate(
                [rows[:, 2 * pair, nope:], rows[:, 2 * pair + 1, nope:]], axis=-1
            )

    return pl.pallas_call(
        kernel,
        out_shape=jax.ShapeDtypeStruct((slabs, tokens, LANES), query.dtype),
        in_specs=[WHOLE],
        out_specs=WHOLE,
        cost_estimate=cost(0, 2 * slabs * tokens * LANES * 2),
        compiler_params=pltpu.CompilerParams(vmem_limit_bytes=4 * MIB),
        name="pack_queries",
    )(query)


def project(section_in, w_down, pieces):
    tokens, depth = section_in.shape
    width = w_down.shape[-1]
    padded = -(-width // LANES) * LANES
    rows = tokens // pieces

    def kernel(in_ref, down_ref, out_ref):
        value = jnp.dot(in_ref[...], down_ref[...], preferred_element_type=jnp.float32)
        out_ref[:, :, :width] = value.reshape(pieces, rows, width)
        out_ref[:, :, width:] = jnp.zeros((pieces, rows, padded - width), jnp.float32)

    return pl.pallas_call(
        kernel,
        out_shape=jax.ShapeDtypeStruct((pieces, rows, padded), jnp.float32),
        in_specs=[WHOLE, WHOLE],
        out_specs=WHOLE,
        cost_estimate=cost(2 * tokens * depth * width, tokens * padded * 4),
        compiler_params=pltpu.CompilerParams(vmem_limit_bytes=6 * MIB),
        name="project",
    )(section_in, w_down)


def norm_rows(pieces, gain, copies):
    parts, rows, width = pieces.shape
    latent = gain.shape[-1]

    def kernel(pieces_ref, gain_ref, out_ref):
        raw = pieces_ref[0]
        for part in range(1, parts):
            raw = raw + pieces_ref[part]
        latent_part = raw[:, :latent]
        mean_sq = jnp.mean(latent_part * latent_part, axis=-1, keepdims=True)
        normed = latent_part * lax.rsqrt(mean_sq + 1e-06) * gain_ref[...]
        row = jnp.concatenate([normed, raw[:, latent:]], axis=-1).astype(jnp.bfloat16)
        for copy in range(copies):
            out_ref[copy] = row

    return pl.pallas_call(
        kernel,
        out_shape=jax.ShapeDtypeStruct((copies, rows, latent + LANES), jnp.bfloat16),
        in_specs=[WHOLE, WHOLE],
        out_specs=WHOLE,
        cost_estimate=cost(0, parts * rows * width * 8),
        compiler_params=pltpu.CompilerParams(vmem_limit_bytes=4 * MIB),
        name="norm_rows",
    )(pieces, gain)


def absorb(block_ids, place, slabs, key_up):
    share = len(slabs)
    _, tokens, _ = slabs[0].shape
    heads, _, latent = key_up.shape
    half = tokens // 2
    n_blocks = block_ids.shape[0]

    def kernel(ids_ref, place_ref, *refs):
        slab_refs, up_ref, out_ref = refs[:share], refs[share], refs[share + 1]
        for back, slab_ref in enumerate(slab_refs):
            owner = place_ref[0] + lax.rem(place_ref[1] + share - back, share) * place_ref[2]
            first = (ids_ref[2 * owner] >= n_blocks // 2).astype(jnp.int32)
            for head in range(heads):
                value = jnp.dot(
                    slab_ref[head], up_ref[head], preferred_element_type=jnp.float32
                ).astype(jnp.bfloat16)
                rope = slab_ref[heads + head // 2]
                if head % 2:
                    rope = jnp.concatenate(
                        [rope[:, LANES // 2 :], rope[:, : LANES // 2]], axis=-1
                    )
                rows = pl.ds(head * half, half)
                out_ref[back, first, rows, :latent] = value[:half]
                out_ref[back, 1 - first, rows, :latent] = value[half:]
                out_ref[back, first, rows, latent:] = rope[:half]
                out_ref[back, 1 - first, rows, latent:] = rope[half:]

    return pl.pallas_call(
        kernel,
        out_shape=jax.ShapeDtypeStruct(
            (share, 2, heads * half, latent + LANES), jnp.bfloat16
        ),
        in_specs=[SCALARS, SCALARS] + [WHOLE] * (share + 1),
        out_specs=WHOLE,
        cost_estimate=cost(
            2 * share * heads * tokens * LANES * latent,
            share * heads * tokens * (latent + LANES) * 4,
        ),
        compiler_params=pltpu.CompilerParams(vmem_limit_bytes=6 * MIB),
        name="absorb",
    )(block_ids, place, *slabs, key_up)


def attend(block_ids, place, query_full, keys, value_up, scale):
    share, _, rows, width = query_full.shape
    sources, tokens, _ = keys.shape
    heads, latent, value_dim = value_up.shape
    half = tokens // 2
    n_blocks = block_ids.shape[0]
    n_keys = sources * half
    factor = scale * LOG2_E

    def kernel(ids_ref, place_ref, query_ref, keys_ref, up_ref, out_ref, turned, plain, held, key_pos):
        step = pl.program_id(0)

        @pl.when(step == 0)
        def _():
            spot = lax.broadcasted_iota(jnp.int32, (8, n_keys), 1)
            low_pos = spot
            for source in range(sources):
                owner = place_ref[1] * sources + source
                id_first = ids_ref[2 * owner]
                first = (id_first >= n_blocks // 2).astype(jnp.int32)
                low_id = jnp.minimum(id_first, n_blocks - 1 - id_first)
                low_pos = jnp.where(
                    spot // half == source, low_id * half + spot % half, low_pos
                )
                for side in range(2):
                    begin = jnp.where(first == side, 0, half)
                    begin = pl.multiple_of(begin, half)
                    plain[side, pl.ds(source * half, half), :] = keys_ref[
                        source, pl.ds(begin, half), :
                    ]
            key_pos[0] = low_pos
            low_block = low_pos // half
            key_pos[1] = (n_blocks - 1 - low_block) * half + low_pos % half
            for side in range(2):
                turned[side] = plain[side].T

        receiver = lax.rem(place_ref[1] + share - step, share)
        id_first = ids_ref[2 * (place_ref[0] + receiver * sources)]
        low_id = jnp.minimum(id_first, n_blocks - 1 - id_first)
        within = lax.broadcasted_iota(jnp.int32, (rows, 1), 0) % half

        def score(side, key_side):
            return (
                jnp.dot(query_ref[0, side], turned[key_side], preferred_element_type=jnp.float32)
                * factor
            )

        def masked(side, block):
            seen = key_pos[side, 0:1, :] <= block * half + within
            return jnp.where(seen, score(side, side), LOW)

        def weigh(expo, key_side):
            return jnp.dot(
                expo.astype(jnp.bfloat16),
                plain[key_side, :, :latent],
                preferred_element_type=jnp.float32,
            )

        lane = lax.broadcasted_iota(jnp.int32, (half, LANES), 1)

        def finish(side, top, total, weighted):
            value = (weighted * (1.0 / total)).astype(jnp.bfloat16)
            level = jnp.where(top > 0.5 * LOW, top + jnp.log2(total), LOW)
            high = level.astype(jnp.bfloat16).astype(jnp.float32)
            rest = level - high
            middle = rest.astype(jnp.bfloat16).astype(jnp.float32)
            parts = (high, middle, rest - middle)
            tile = jnp.zeros((half, LANES), jnp.float32)
            for head in range(heads):
                span = slice(head * half, (head + 1) * half)
                row = pl.multiple_of(receiver * tokens + side * half, half)
                held[head, pl.ds(row, half), :] = value[span]
                for at, part in enumerate(parts):
                    tile = jnp.where(lane == 3 * head + at, part[span], tile)
            out_ref[receiver, pl.ds(side * half, half), heads * value_dim :] = tile.astype(jnp.bfloat16)

        low_low = masked(0, low_id)
        high_low = score(1, 0)
        high_high = masked(1, n_blocks - 1 - low_id)
        top_low = jnp.max(low_low, axis=1, keepdims=True)
        top_high = jnp.maximum(
            jnp.max(high_low, axis=1, keepdims=True), jnp.max(high_high, axis=1, keepdims=True)
        )
        low_low = jnp.exp2(low_low - top_low)
        high_low = jnp.exp2(high_low - top_high)
        high_high = jnp.exp2(high_high - top_high)
        total_low = jnp.sum(low_low, axis=1, keepdims=True)
        total_high = jnp.sum(high_low, axis=1, keepdims=True) + jnp.sum(
            high_high, axis=1, keepdims=True
        )
        finish(0, top_low, total_low, weigh(low_low, 0))
        finish(1, top_high, total_high, weigh(high_low, 0) + weigh(high_high, 1))

        @pl.when(step == share - 1)
        def _():
            for head in range(heads):
                value = jnp.dot(held[head], up_ref[head], preferred_element_type=jnp.float32)
                out_ref[:, :, head * value_dim : (head + 1) * value_dim] = value.astype(
                    jnp.bfloat16
                ).reshape(share, tokens, value_dim)

    out_width = heads * value_dim + LANES
    return pl.pallas_call(
        kernel,
        out_shape=jax.ShapeDtypeStruct((share, tokens, out_width), jnp.bfloat16),
        grid=(share,),
        in_specs=[
            SCALARS,
            SCALARS,
            pl.BlockSpec((1, 2, rows, width), lambda g: (g, 0, 0, 0)),
            pl.BlockSpec((sources, tokens, width), lambda g: (0, 0, 0)),
            pl.BlockSpec((heads, latent, value_dim), lambda g: (0, 0, 0)),
        ],
        out_specs=pl.BlockSpec((share, tokens, out_width), lambda g: (0, 0, 0)),
        scratch_shapes=[
            pltpu.VMEM((2, width, n_keys), jnp.bfloat16),
            pltpu.VMEM((2, n_keys, width), jnp.bfloat16),
            pltpu.VMEM((heads, share * tokens, latent), jnp.bfloat16),
            pltpu.VMEM((2, 8, n_keys), jnp.int32),
        ],
        cost_estimate=cost(
            share * 6 * rows * n_keys * (width + latent), share * rows * width * 4
        ),
        compiler_params=pltpu.CompilerParams(vmem_limit_bytes=24 * MIB),
        name="attend",
    )(block_ids, place, query_full, keys, value_up)


def combine(block_ids, place, parts, heads):
    share, tokens, width = parts.shape
    value_width = width - LANES
    value_dim = value_width // heads
    half = tokens // 2
    n_blocks = block_ids.shape[0]

    def kernel(ids_ref, place_ref, parts_ref, out_ref):
        first = (ids_ref[2 * (place_ref[0] + place_ref[1] * place_ref[2])] >= n_blocks // 2).astype(jnp.int32)
        for side in range(2):
            begin = pl.multiple_of(jnp.where(first == side, 0, half), half)
            span = slice(side * half, (side + 1) * half)
            stats = [parts_ref[k, span, value_width:].astype(jnp.float32) for k in range(share)]
            for head in range(heads):
                levels = [
                    s[:, 3 * head : 3 * head + 1]
                    + s[:, 3 * head + 1 : 3 * head + 2]
                    + s[:, 3 * head + 2 : 3 * head + 3]
                    for s in stats
                ]
                top = functools.reduce(jnp.maximum, levels)
                shares = [jnp.exp2(level - top) for level in levels]
                inverse = 1.0 / functools.reduce(jnp.add, shares)
                columns = slice(head * value_dim, (head + 1) * value_dim)
                value = jnp.zeros((half, value_dim), jnp.float32)
                for k in range(share):
                    value += parts_ref[k, span, columns].astype(jnp.float32) * (
                        shares[k] * inverse
                    )
                out_ref[0, pl.ds(begin, half), columns] = value.astype(jnp.bfloat16)

    return pl.pallas_call(
        kernel,
        out_shape=jax.ShapeDtypeStruct((1, tokens, value_width), jnp.bfloat16),
        in_specs=[SCALARS, SCALARS, WHOLE],
        out_specs=WHOLE,
        cost_estimate=cost(0, share * tokens * width * 2),
        compiler_params=pltpu.CompilerParams(vmem_limit_bytes=6 * MIB),
        name="combine",
    )(block_ids, place, parts)


def shards(outgoing, w_down, kv_gain, queries, w_key_up, w_value_up, block_ids):
    section_idx = lax.axis_index("pp")
    n_share, n_y0, n_x, tp_size = (lax.axis_size(a) for a in (SHARE, *KEYS, "tp"))
    n_keys = n_y0 * n_x
    tokens, heads, query_dim = queries.shape[1:]
    y1, y0, x = (lax.axis_index(a).astype(jnp.int32) for a in CTX)
    place = jnp.stack([y0 * n_x + x, y1, jnp.int32(n_keys)])

    moved = lax.ppermute(outgoing, "pp", [(0, 1)])
    section_in = jnp.where(section_idx == 0, outgoing, moved)[0]
    partial_value = project(section_in, w_down[0], tp_size)
    pieces = exchange(partial_value, ("tp",))
    slabs = [pack_queries(queries[0])]
    for ahead in range(1, n_share):
        pairs = [(i, (i + ahead) % n_share) for i in range(n_share)]
        slabs.append(lax.ppermute(slabs[0], SHARE, pairs))
    local = norm_rows(pieces, kv_gain, tp_size)
    key_rows = exchange(local, ("tp",)).reshape(tokens, -1)
    query_full = absorb(block_ids, place, slabs, w_key_up[0])
    keys = exchange(jnp.broadcast_to(key_rows, (n_keys, *key_rows.shape)), KEYS)
    part_out = attend(block_ids, place, query_full, keys, w_value_up[0], query_dim**-0.5)
    got = exchange(part_out, (SHARE,))
    return combine(block_ids, place, got, heads)


def build(torus):
    placed = (
        P("pp", CTX, "tp"),
        P("pp", "tp", None),
        P("pp", None),
        P("pp", CTX, "tp", None),
        P("pp", "tp", None, None),
        P("pp", "tp", None, None),
        P(),
    )
    return jax.shard_map(
        shards, mesh=torus, in_specs=placed, out_specs=P("pp", CTX, "tp"), check_vma=False
    )


def solution(mesh):
    torus = Mesh(
        mesh.devices.reshape(4, 2, 4, mesh.shape["pp"], mesh.shape["tp"]),
        ("y1", "y0", "x", "pp", "tp"),
    )
    return build(torus)
```

```python
import functools

import jax
import jax.numpy as jnp
from jax import lax
from jax.experimental import pallas as pl
from jax.experimental.layout import Layout, with_layout_constraint
from jax.experimental.pallas import tpu as pltpu
from jax.sharding import Mesh
from jax.sharding import PartitionSpec as P

CTX = ("y1", "y0", "x")
SHARE = "y1"
KEYS = ("y0", "x")
LANES = 128
SUBLANES = 8
LOG2_E = 1.4426950408889634
LOW = -1e30
MIB = 1 << 20
WHOLE = pl.BlockSpec(memory_space=pltpu.VMEM)
SCALARS = pl.BlockSpec(memory_space=pltpu.SMEM)


def exchange(array, axes):
    return lax.all_to_all(array, axes, 0, 0, tiled=True)


def cost(flops, bytes_accessed):
    return pl.CostEstimate(flops=flops, bytes_accessed=bytes_accessed, transcendentals=0)


def norm_rows(pieces, gain, copies):
    parts, rows, width = pieces.shape
    latent = gain.shape[-1]

    def kernel(pieces_ref, gain_ref, out_ref):
        raw = pieces_ref[0]
        for part in range(1, parts):
            raw = raw + pieces_ref[part]
        latent_part = raw[:, :latent]
        mean_sq = jnp.mean(latent_part * latent_part, axis=-1, keepdims=True)
        normed = latent_part * lax.rsqrt(mean_sq + 1e-06) * gain_ref[...]
        row = jnp.concatenate([normed, raw[:, latent:]], axis=-1).astype(jnp.bfloat16)
        for copy in range(copies):
            out_ref[copy] = row

    return pl.pallas_call(
        kernel,
        out_shape=jax.ShapeDtypeStruct((copies, rows, latent + LANES), jnp.bfloat16),
        in_specs=[WHOLE, WHOLE],
        out_specs=WHOLE,
        cost_estimate=cost(0, parts * rows * width * 8),
        compiler_params=pltpu.CompilerParams(vmem_limit_bytes=4 * MIB),
        name="norm_rows",
    )(pieces, gain)


def absorb(block_ids, place, slabs, key_up):
    share = len(slabs)
    _, query_dim, tokens = slabs[0].shape
    heads, nope, latent = key_up.shape
    half = tokens // 2
    n_blocks = block_ids.shape[0]

    def kernel(ids_ref, place_ref, *refs):
        slab_refs, up_ref, out_ref = refs[:share], refs[share], refs[share + 1]
        for back, slab_ref in enumerate(slab_refs):
            owner = place_ref[0] + lax.rem(place_ref[1] + share - back, share) * place_ref[2]
            first = (ids_ref[2 * owner] >= n_blocks // 2).astype(jnp.int32)
            for head in range(heads):
                value = lax.dot_general(
                    slab_ref[head, :nope],
                    up_ref[head],
                    (((0,), (0,)), ((), ())),
                    preferred_element_type=jnp.float32,
                ).astype(jnp.bfloat16)
                rope = jnp.concatenate(
                    [
                        slab_ref[head, nope:].T,
                        jnp.zeros((tokens, LANES - (query_dim - nope)), jnp.bfloat16),
                    ],
                    axis=-1,
                )
                rows = pl.ds(head * half, half)
                out_ref[back, first, rows, :latent] = value[:half]
                out_ref[back, 1 - first, rows, :latent] = value[half:]
                out_ref[back, first, rows, latent:] = rope[:half]
                out_ref[back, 1 - first, rows, latent:] = rope[half:]

    return pl.pallas_call(
        kernel,
        out_shape=jax.ShapeDtypeStruct(
            (share, 2, heads * half, latent + LANES), jnp.bfloat16
        ),
        in_specs=[SCALARS, SCALARS] + [WHOLE] * (share + 1),
        out_specs=WHOLE,
        cost_estimate=cost(
            2 * share * heads * tokens * LANES * latent,
            share * heads * tokens * (latent + LANES) * 4,
        ),
        compiler_params=pltpu.CompilerParams(vmem_limit_bytes=6 * MIB),
        name="absorb",
    )(block_ids, place, *slabs, key_up)


def attend(block_ids, place, query_full, keys, value_up, scale):
    share, _, rows, width = query_full.shape
    sources, tokens, _ = keys.shape
    heads, latent, value_dim = value_up.shape
    half = tokens // 2
    n_blocks = block_ids.shape[0]
    n_keys = sources * half
    factor = scale * LOG2_E

    def kernel(ids_ref, place_ref, query_ref, keys_ref, up_ref, out_ref, turned, plain, held, key_pos):
        step = pl.program_id(0)

        @pl.when(step == 0)
        def _():
            spot = lax.broadcasted_iota(jnp.int32, (8, n_keys), 1)
            low_pos = spot
            for source in range(sources):
                owner = place_ref[1] * sources + source
                id_first = ids_ref[2 * owner]
                first = (id_first >= n_blocks // 2).astype(jnp.int32)
                low_id = jnp.minimum(id_first, n_blocks - 1 - id_first)
                low_pos = jnp.where(
                    spot // half == source, low_id * half + spot % half, low_pos
                )
                for side in range(2):
                    begin = jnp.where(first == side, 0, half)
                    begin = pl.multiple_of(begin, half)
                    plain[side, pl.ds(source * half, half), :] = keys_ref[
                        source, pl.ds(begin, half), :
                    ]
            key_pos[0] = low_pos
            low_block = low_pos // half
            key_pos[1] = (n_blocks - 1 - low_block) * half + low_pos % half
            for side in range(2):
                turned[side] = plain[side].T

        receiver = lax.rem(place_ref[1] + share - step, share)
        id_first = ids_ref[2 * (place_ref[0] + receiver * sources)]
        low_id = jnp.minimum(id_first, n_blocks - 1 - id_first)
        within = lax.broadcasted_iota(jnp.int32, (rows, 1), 0) % half

        def score(side, key_side):
            return (
                jnp.dot(query_ref[0, side], turned[key_side], preferred_element_type=jnp.float32)
                * factor
            )

        def masked(side, block):
            seen = key_pos[side, 0:1, :] <= block * half + within
            return jnp.where(seen, score(side, side), LOW)

        def weigh(expo, key_side):
            return jnp.dot(
                expo.astype(jnp.bfloat16),
                plain[key_side, :, :latent],
                preferred_element_type=jnp.float32,
            )

        lane = lax.broadcasted_iota(jnp.int32, (half, LANES), 1)

        def finish(side, top, total, weighted):
            value = (weighted * (1.0 / total)).astype(jnp.bfloat16)
            level = jnp.where(top > 0.5 * LOW, top + jnp.log2(total), LOW)
            high = level.astype(jnp.bfloat16).astype(jnp.float32)
            rest = level - high
            middle = rest.astype(jnp.bfloat16).astype(jnp.float32)
            parts = (high, middle, rest - middle)
            tile = jnp.zeros((half, LANES), jnp.float32)
            for head in range(heads):
                span = slice(head * half, (head + 1) * half)
                row = pl.multiple_of(receiver * tokens + side * half, half)
                held[head, pl.ds(row, half), :] = value[span]
                for at, part in enumerate(parts):
                    tile = jnp.where(lane == SUBLANES * head + at, part[span], tile)
            return tile

        low_low = masked(0, low_id)
        high_low = score(1, 0)
        high_high = masked(1, n_blocks - 1 - low_id)
        top_low = jnp.max(low_low, axis=1, keepdims=True)
        top_high = jnp.maximum(
            jnp.max(high_low, axis=1, keepdims=True), jnp.max(high_high, axis=1, keepdims=True)
        )
        low_low = jnp.exp2(low_low - top_low)
        high_low = jnp.exp2(high_low - top_high)
        high_high = jnp.exp2(high_high - top_high)
        total_low = jnp.sum(low_low, axis=1, keepdims=True)
        total_high = jnp.sum(high_low, axis=1, keepdims=True) + jnp.sum(
            high_high, axis=1, keepdims=True
        )
        tiles = (
            finish(0, top_low, total_low, weigh(low_low, 0)),
            finish(1, top_high, total_high, weigh(high_low, 0) + weigh(high_high, 1)),
        )
        levels = jnp.concatenate(tiles, axis=0).T
        for head in range(heads):
            out_ref[receiver, tokens:, head * tokens : (head + 1) * tokens] = levels[
                head * SUBLANES : (head + 1) * SUBLANES
            ].astype(jnp.bfloat16)

        @pl.when(step == share - 1)
        def _():
            for head in range(heads):
                value = jnp.dot(held[head], up_ref[head], preferred_element_type=jnp.float32)
                out_ref[:, :tokens, head * value_dim : (head + 1) * value_dim] = value.astype(
                    jnp.bfloat16
                ).reshape(share, tokens, value_dim)

    out_width = heads * value_dim
    return pl.pallas_call(
        kernel,
        out_shape=jax.ShapeDtypeStruct((share, tokens + SUBLANES, out_width), jnp.bfloat16),
        grid=(share,),
        in_specs=[
            SCALARS,
            SCALARS,
            pl.BlockSpec((1, 2, rows, width), lambda g: (g, 0, 0, 0)),
            pl.BlockSpec((sources, tokens, width), lambda g: (0, 0, 0)),
            pl.BlockSpec((heads, latent, value_dim), lambda g: (0, 0, 0)),
        ],
        out_specs=pl.BlockSpec((share, tokens + SUBLANES, out_width), lambda g: (0, 0, 0)),
        scratch_shapes=[
            pltpu.VMEM((2, width, n_keys), jnp.bfloat16),
            pltpu.VMEM((2, n_keys, width), jnp.bfloat16),
            pltpu.VMEM((heads, share * tokens, latent), jnp.bfloat16),
            pltpu.VMEM((2, 8, n_keys), jnp.int32),
        ],
        cost_estimate=cost(
            share * 6 * rows * n_keys * (width + latent), share * rows * width * 4
        ),
        compiler_params=pltpu.CompilerParams(vmem_limit_bytes=24 * MIB),
        name="attend",
    )(block_ids, place, query_full, keys, value_up)


def combine(block_ids, place, parts, heads):
    share, rows, width = parts.shape
    tokens = rows - SUBLANES
    value_dim = width // heads
    half = tokens // 2
    n_blocks = block_ids.shape[0]

    def kernel(ids_ref, place_ref, parts_ref, out_ref):
        owner = place_ref[0] + place_ref[1] * place_ref[2]
        first = (ids_ref[2 * owner] >= n_blocks // 2).astype(jnp.int32)
        shares = []
        for head in range(heads):
            levels = []
            for k in range(share):
                stat = parts_ref[k, tokens:, head * tokens : (head + 1) * tokens].astype(
                    jnp.float32
                )
                levels.append(stat[0:1] + stat[1:2] + stat[2:3])
            top = functools.reduce(jnp.maximum, levels)
            weights = [jnp.exp2(level - top) for level in levels]
            inverse = 1.0 / functools.reduce(jnp.add, weights)
            shares += [weight * inverse for weight in weights]
        shares += [jnp.zeros((1, tokens), jnp.float32)] * (LANES - len(shares))
        turned = jnp.concatenate(shares, axis=0).T
        for side in range(2):
            begin = pl.multiple_of(jnp.where(first == side, 0, half), half)
            span = slice(side * half, (side + 1) * half)
            for head in range(heads):
                columns = slice(head * value_dim, (head + 1) * value_dim)
                value = jnp.zeros((half, value_dim), jnp.float32)
                for k in range(share):
                    at = head * share + k
                    value += parts_ref[k, span, columns].astype(jnp.float32) * (
                        turned[span, at : at + 1]
                    )
                out_ref[0, pl.ds(begin, half), columns] = value.astype(jnp.bfloat16)

    return pl.pallas_call(
        kernel,
        out_shape=jax.ShapeDtypeStruct((1, tokens, width), jnp.bfloat16),
        in_specs=[SCALARS, SCALARS, WHOLE],
        out_specs=WHOLE,
        cost_estimate=cost(0, share * tokens * width * 2),
        compiler_params=pltpu.CompilerParams(vmem_limit_bytes=6 * MIB),
        name="combine",
    )(block_ids, place, parts)


def shards(outgoing, w_down, kv_gain, queries, w_key_up, w_value_up, block_ids):
    section_idx = lax.axis_index("pp")
    rows_first = Layout(major_to_minor=(0, 1))
    hidden = with_layout_constraint(outgoing[0].T, rows_first)
    n_share, n_y0, n_x, tp_size = (lax.axis_size(a) for a in (SHARE, *KEYS, "tp"))
    n_keys = n_y0 * n_x
    tokens, heads, query_dim = queries.shape[1:]
    y1, y0, x = (lax.axis_index(a).astype(jnp.int32) for a in CTX)
    place = jnp.stack([y0 * n_x + x, y1, jnp.int32(n_keys)])

    moved = with_layout_constraint(lax.ppermute(hidden, "pp", [(0, 1)]), rows_first)
    section_in = jnp.where(section_idx == 0, hidden, moved)
    partial_value = lax.dot_general(
        section_in,
        w_down[0],
        (((0,), (0,)), ((), ())),
        preferred_element_type=jnp.float32,
    ).reshape(tp_size, tokens // tp_size, -1)
    spare = -partial_value.shape[-1] % LANES
    partial_value = jnp.pad(partial_value, ((0, 0), (0, 0), (0, spare)))
    pieces = exchange(partial_value, ("tp",))
    slabs = [queries[0].transpose(1, 2, 0)]
    for ahead in range(1, n_share):
        pairs = [(i, (i + ahead) % n_share) for i in range(n_share)]
        slabs.append(lax.ppermute(slabs[0], SHARE, pairs))
    local = norm_rows(pieces, kv_gain, tp_size)
    key_rows = exchange(local, ("tp",)).reshape(tokens, -1)
    query_full = absorb(block_ids, place, slabs, w_key_up[0])
    keys = exchange(jnp.broadcast_to(key_rows, (n_keys, *key_rows.shape)), KEYS)
    part_out = attend(block_ids, place, query_full, keys, w_value_up[0], query_dim**-0.5)
    got = exchange(part_out, (SHARE,))
    return combine(block_ids, place, got, heads)


def build(torus):
    placed = (
        P("pp", CTX, "tp"),
        P("pp", "tp", None),
        P("pp", None),
        P("pp", CTX, "tp", None),
        P("pp", "tp", None, None),
        P("pp", "tp", None, None),
        P(),
    )
    return jax.shard_map(
        shards, mesh=torus, in_specs=placed, out_specs=P("pp", CTX, "tp"), check_vma=False
    )


def solution(mesh):
    torus = Mesh(
        mesh.devices.reshape(4, 2, 4, mesh.shape["pp"], mesh.shape["tp"]),
        ("y1", "y0", "x", "pp", "tp"),
    )
    return build(torus)
```

```python
import functools

import jax
import jax.numpy as jnp
from jax import lax
from jax.experimental import pallas as pl
from jax.experimental.layout import Layout, with_layout_constraint
from jax.experimental.pallas import tpu as pltpu
from jax.sharding import Mesh
from jax.sharding import PartitionSpec as P

CTX = ("y1", "y0", "x")
SHARE = "y1"
KEYS = ("y0", "x")
LANES = 128
SUBLANES = 8
LOG2_E = 1.4426950408889634
LOW = -1e30
MIB = 1 << 20
WHOLE = pl.BlockSpec(memory_space=pltpu.VMEM)
SCALARS = pl.BlockSpec(memory_space=pltpu.SMEM)


def exchange(array, axes):
    return lax.all_to_all(array, axes, 0, 0, tiled=True)


def cost(flops, bytes_accessed):
    return pl.CostEstimate(flops=flops, bytes_accessed=bytes_accessed, transcendentals=0)


def norm_rows(pieces, gain, copies):
    parts, rows, width = pieces.shape
    latent = gain.shape[-1]

    def kernel(pieces_ref, gain_ref, out_ref):
        raw = pieces_ref[0]
        for part in range(1, parts):
            raw = raw + pieces_ref[part]
        latent_part = raw[:, :latent]
        mean_sq = jnp.mean(latent_part * latent_part, axis=-1, keepdims=True)
        normed = latent_part * lax.rsqrt(mean_sq + 1e-06) * gain_ref[...]
        spare = jnp.zeros((rows, latent + LANES - width), jnp.float32)
        row = jnp.concatenate([normed, raw[:, latent:], spare], axis=-1).astype(jnp.bfloat16)
        for copy in range(copies):
            out_ref[copy] = row

    return pl.pallas_call(
        kernel,
        out_shape=jax.ShapeDtypeStruct((copies, rows, latent + LANES), jnp.bfloat16),
        in_specs=[WHOLE, WHOLE],
        out_specs=WHOLE,
        cost_estimate=cost(0, parts * rows * width * 8),
        compiler_params=pltpu.CompilerParams(vmem_limit_bytes=4 * MIB),
        name="norm_rows",
    )(pieces, gain)


def absorb(block_ids, place, slabs, key_up):
    share = len(slabs)
    _, query_dim, tokens = slabs[0].shape
    heads, nope, latent = key_up.shape
    half = tokens // 2
    n_blocks = block_ids.shape[0]

    def kernel(ids_ref, place_ref, *refs):
        slab_refs, up_ref, out_ref = refs[:share], refs[share], refs[share + 1]
        for back, slab_ref in enumerate(slab_refs):
            owner = place_ref[0] + lax.rem(place_ref[1] + share - back, share) * place_ref[2]
            first = (ids_ref[2 * owner] >= n_blocks // 2).astype(jnp.int32)
            for head in range(heads):
                value = lax.dot_general(
                    slab_ref[head, :nope],
                    up_ref[head],
                    (((0,), (0,)), ((), ())),
                    preferred_element_type=jnp.float32,
                ).astype(jnp.bfloat16)
                rope = jnp.concatenate(
                    [
                        slab_ref[head, nope:].T,
                        jnp.zeros((tokens, LANES - (query_dim - nope)), jnp.bfloat16),
                    ],
                    axis=-1,
                )
                rows = pl.ds(head * half, half)
                out_ref[back, first, rows, :latent] = value[:half]
                out_ref[back, 1 - first, rows, :latent] = value[half:]
                out_ref[back, first, rows, latent:] = rope[:half]
                out_ref[back, 1 - first, rows, latent:] = rope[half:]

    return pl.pallas_call(
        kernel,
        out_shape=jax.ShapeDtypeStruct(
            (share, 2, heads * half, latent + LANES), jnp.bfloat16
        ),
        in_specs=[SCALARS, SCALARS] + [WHOLE] * (share + 1),
        out_specs=WHOLE,
        cost_estimate=cost(
            2 * share * heads * tokens * LANES * latent,
            share * heads * tokens * (latent + LANES) * 4,
        ),
        compiler_params=pltpu.CompilerParams(vmem_limit_bytes=6 * MIB),
        name="absorb",
    )(block_ids, place, *slabs, key_up)


def attend(block_ids, place, query_full, keys, value_up, scale):
    share, _, rows, width = query_full.shape
    sources, tokens, _ = keys.shape
    heads, latent, value_dim = value_up.shape
    half = tokens // 2
    n_blocks = block_ids.shape[0]
    n_keys = sources * half
    factor = scale * LOG2_E

    def kernel(ids_ref, place_ref, query_ref, keys_ref, up_ref, out_ref, plain, held, key_pos):
        step = pl.program_id(0)

        @pl.when(step == 0)
        def _():
            spot = lax.broadcasted_iota(jnp.int32, (8, n_keys), 1)
            low_pos = spot
            for source in range(sources):
                owner = place_ref[1] * sources + source
                id_first = ids_ref[2 * owner]
                first = (id_first >= n_blocks // 2).astype(jnp.int32)
                low_id = jnp.minimum(id_first, n_blocks - 1 - id_first)
                low_pos = jnp.where(
                    spot // half == source, low_id * half + spot % half, low_pos
                )
                for side in range(2):
                    begin = jnp.where(first == side, 0, half)
                    begin = pl.multiple_of(begin, half)
                    plain[side, pl.ds(source * half, half), :] = keys_ref[
                        source, pl.ds(begin, half), :
                    ]
            key_pos[0] = low_pos
            low_block = low_pos // half
            key_pos[1] = (n_blocks - 1 - low_block) * half + low_pos % half

        receiver = lax.rem(place_ref[1] + share - step, share)
        id_first = ids_ref[2 * (place_ref[0] + receiver * sources)]
        low_id = jnp.minimum(id_first, n_blocks - 1 - id_first)
        within = lax.broadcasted_iota(jnp.int32, (rows, 1), 0) % half

        def score(side, key_side):
            return (
                lax.dot_general(
                    query_ref[0, side],
                    plain[key_side],
                    (((1,), (1,)), ((), ())),
                    preferred_element_type=jnp.float32,
                )
                * factor
            )

        def masked(side, block):
            seen = key_pos[side, 0:1, :] <= block * half + within
            return jnp.where(seen, score(side, side), LOW)

        def weigh(expo, key_side):
            return jnp.dot(
                expo.astype(jnp.bfloat16),
                plain[key_side, :, :latent],
                preferred_element_type=jnp.float32,
            )

        lane = lax.broadcasted_iota(jnp.int32, (half, LANES), 1)

        def finish(side, top, total, weighted):
            value = (weighted * (1.0 / total)).astype(jnp.bfloat16)
            level = jnp.where(top > 0.5 * LOW, top + jnp.log2(total), LOW)
            high = level.astype(jnp.bfloat16).astype(jnp.float32)
            rest = level - high
            middle = rest.astype(jnp.bfloat16).astype(jnp.float32)
            parts = (high, middle, rest - middle)
            tile = jnp.zeros((half, LANES), jnp.float32)
            for head in range(heads):
                span = slice(head * half, (head + 1) * half)
                row = pl.multiple_of(receiver * tokens + side * half, half)
                held[head, pl.ds(row, half), :] = value[span]
                for at, part in enumerate(parts):
                    tile = jnp.where(lane == SUBLANES * head + at, part[span], tile)
            return tile

        low_low = masked(0, low_id)
        high_low = score(1, 0)
        high_high = masked(1, n_blocks - 1 - low_id)
        top_low = jnp.max(low_low, axis=1, keepdims=True)
        top_high = jnp.maximum(
            jnp.max(high_low, axis=1, keepdims=True), jnp.max(high_high, axis=1, keepdims=True)
        )
        low_low = jnp.exp2(low_low - top_low)
        high_low = jnp.exp2(high_low - top_high)
        high_high = jnp.exp2(high_high - top_high)
        total_low = jnp.sum(low_low, axis=1, keepdims=True)
        total_high = jnp.sum(high_low, axis=1, keepdims=True) + jnp.sum(
            high_high, axis=1, keepdims=True
        )
        tiles = (
            finish(0, top_low, total_low, weigh(low_low, 0)),
            finish(1, top_high, total_high, weigh(high_low, 0) + weigh(high_high, 1)),
        )
        levels = jnp.concatenate(tiles, axis=0).T
        for head in range(heads):
            out_ref[receiver, tokens:, head * tokens : (head + 1) * tokens] = levels[
                head * SUBLANES : (head + 1) * SUBLANES
            ].astype(jnp.bfloat16)

        @pl.when(step == share - 1)
        def _():
            for head in range(heads):
                value = jnp.dot(held[head], up_ref[head], preferred_element_type=jnp.float32)
                out_ref[:, :tokens, head * value_dim : (head + 1) * value_dim] = value.astype(
                    jnp.bfloat16
                ).reshape(share, tokens, value_dim)

    out_width = heads * value_dim
    return pl.pallas_call(
        kernel,
        out_shape=jax.ShapeDtypeStruct((share, tokens + SUBLANES, out_width), jnp.bfloat16),
        grid=(share,),
        in_specs=[
            SCALARS,
            SCALARS,
            pl.BlockSpec((1, 2, rows, width), lambda g: (g, 0, 0, 0)),
            pl.BlockSpec((sources, tokens, width), lambda g: (0, 0, 0)),
            pl.BlockSpec((heads, latent, value_dim), lambda g: (0, 0, 0)),
        ],
        out_specs=pl.BlockSpec((share, tokens + SUBLANES, out_width), lambda g: (0, 0, 0)),
        scratch_shapes=[
            pltpu.VMEM((2, n_keys, width), jnp.bfloat16),
            pltpu.VMEM((heads, share * tokens, latent), jnp.bfloat16),
            pltpu.VMEM((2, 8, n_keys), jnp.int32),
        ],
        cost_estimate=cost(
            share * 6 * rows * n_keys * (width + latent), share * rows * width * 4
        ),
        compiler_params=pltpu.CompilerParams(vmem_limit_bytes=24 * MIB),
        name="attend",
    )(block_ids, place, query_full, keys, value_up)


def combine(block_ids, place, parts, heads):
    share, rows, width = parts.shape
    tokens = rows - SUBLANES
    value_dim = width // heads
    half = tokens // 2
    n_blocks = block_ids.shape[0]

    def kernel(ids_ref, place_ref, parts_ref, out_ref):
        owner = place_ref[0] + place_ref[1] * place_ref[2]
        first = (ids_ref[2 * owner] >= n_blocks // 2).astype(jnp.int32)
        shares = []
        for head in range(heads):
            levels = []
            for k in range(share):
                stat = parts_ref[k, tokens:, head * tokens : (head + 1) * tokens].astype(
                    jnp.float32
                )
                levels.append(stat[0:1] + stat[1:2] + stat[2:3])
            top = functools.reduce(jnp.maximum, levels)
            weights = [jnp.exp2(level - top) for level in levels]
            inverse = 1.0 / functools.reduce(jnp.add, weights)
            shares += [weight * inverse for weight in weights]
        shares += [jnp.zeros((1, tokens), jnp.float32)] * (LANES - len(shares))
        turned = jnp.concatenate(shares, axis=0).T
        for side in range(2):
            begin = pl.multiple_of(jnp.where(first == side, 0, half), half)
            span = slice(side * half, (side + 1) * half)
            for head in range(heads):
                columns = slice(head * value_dim, (head + 1) * value_dim)
                value = jnp.zeros((half, value_dim), jnp.float32)
                for k in range(share):
                    at = head * share + k
                    value += parts_ref[k, span, columns].astype(jnp.float32) * (
                        turned[span, at : at + 1]
                    )
                out_ref[0, pl.ds(begin, half), columns] = value.astype(jnp.bfloat16)

    return pl.pallas_call(
        kernel,
        out_shape=jax.ShapeDtypeStruct((1, tokens, width), jnp.bfloat16),
        in_specs=[SCALARS, SCALARS, WHOLE],
        out_specs=WHOLE,
        cost_estimate=cost(0, share * tokens * width * 2),
        compiler_params=pltpu.CompilerParams(vmem_limit_bytes=6 * MIB),
        name="combine",
    )(block_ids, place, parts)


def shards(outgoing, w_down, kv_gain, queries, w_key_up, w_value_up, block_ids):
    section_idx = lax.axis_index("pp")
    rows_first = Layout(major_to_minor=(0, 1))
    hidden = with_layout_constraint(outgoing[0].T, rows_first)
    n_share, n_y0, n_x, tp_size = (lax.axis_size(a) for a in (SHARE, *KEYS, "tp"))
    n_keys = n_y0 * n_x
    tokens, heads, query_dim = queries.shape[1:]
    y1, y0, x = (lax.axis_index(a).astype(jnp.int32) for a in CTX)
    place = jnp.stack([y0 * n_x + x, y1, jnp.int32(n_keys)])

    moved = with_layout_constraint(lax.ppermute(hidden, "pp", [(0, 1)]), rows_first)
    section_in = jnp.where(section_idx == 0, hidden, moved)
    partial_value = lax.dot_general(
        section_in,
        w_down[0],
        (((0,), (0,)), ((), ())),
        preferred_element_type=jnp.float32,
    ).reshape(tp_size, tokens // tp_size, -1)
    pieces = exchange(partial_value, ("tp",))
    slabs = [queries[0].transpose(1, 2, 0)]
    for ahead in range(1, n_share):
        pairs = [(i, (i + ahead) % n_share) for i in range(n_share)]
        slabs.append(lax.ppermute(slabs[0], SHARE, pairs))
    local = norm_rows(pieces, kv_gain, tp_size)
    key_rows = exchange(local, ("tp",)).reshape(tokens, -1)
    query_full = absorb(block_ids, place, slabs, w_key_up[0])
    keys = exchange(jnp.broadcast_to(key_rows, (n_keys, *key_rows.shape)), KEYS)
    part_out = attend(block_ids, place, query_full, keys, w_value_up[0], query_dim**-0.5)
    got = exchange(part_out, (SHARE,))
    return combine(block_ids, place, got, heads)


def build(torus):
    placed = (
        P("pp", CTX, "tp"),
        P("pp", "tp", None),
        P("pp", None),
        P("pp", CTX, "tp", None),
        P("pp", "tp", None, None),
        P("pp", "tp", None, None),
        P(),
    )
    return jax.shard_map(
        shards, mesh=torus, in_specs=placed, out_specs=P("pp", CTX, "tp"), check_vma=False
    )


def solution(mesh):
    torus = Mesh(
        mesh.devices.reshape(4, 2, 4, mesh.shape["pp"], mesh.shape["tp"]),
        ("y1", "y0", "x", "pp", "tp"),
    )
    return build(torus)
```
